1024 devices in a mesh: dp: 16 (over z), section: 8 (over x, core), expert: 8 (over y).
Axes of the slice: x: 4, y: 8, z: 16, core: 2. Of those that a mesh axis runs over, the one named last changes fastest.
Arguments:
- act_in: bfloat16 [8, 8192, 2048], P('section', ('dp', 'expert')), may hold values from -6 to 6
- saved_in: bfloat16 [8, 8192, 2048], P('section', ('dp', 'expert')), may hold values from -6 to 6
- grad_in: bfloat16 [8, 8192, 2048], P('section', ('dp', 'expert')), may hold values from -6 to 6
- fwd_ids: int32 [8, 8192, 2], P('section', ('dp', 'expert')), may hold values from 0 to 7, all different within a row; in each aligned block of 64 rows (0 to 63, 64 to 127, ..., all dimensions but the last counted through in order) at most 20 rows name the same one
- bwd_ids: int32 [8, 8192, 2], P('section', ('dp', 'expert')), may hold values from 0 to 7, all different within a row; in each aligned block of 64 rows (0 to 63, 64 to 127, ..., all dimensions but the last counted through in order) at most 20 rows name the same one
- fwd_gates: float32 [8, 8192, 2], P('section', ('dp', 'expert')), may hold values from 0.2 to 1
- bwd_gates: float32 [8, 8192, 2], P('section', ('dp', 'expert')), may hold values from 0.2 to 1
- norm_gain: float32 [8, 2048], P('section'), may hold values from 0.5 to 1.5
- w_gate: bfloat16 [8, 8, 2048, 384], P('section', 'expert'), may hold values from -0.125 to 0.125
- w_up: bfloat16 [8, 8, 2048, 384], P('section', 'expert'), may hold values from -0.125 to 0.125
- w_down: bfloat16 [8, 8, 384, 2048], P('section', 'expert'), may hold values from -0.3125 to 0.3125
Outputs:
- act_out: bfloat16 [8, 8192, 2048], P('section', ('dp', 'expert'))
- grad_out: bfloat16 [8, 8192, 2048], P('section', ('dp', 'expert'))
- weight_grads: float32 [8, 8, 2048, 1152], P('section', 'expert', 'dp')
The draws below stay inside these ranges and needn't reach their ends.
Inputs may be any that keep to these rules, and one draw needn't show every extreme that they name: `fwd_ids`: the 2 entries of a token name different experts. In each aligned block of 64 tokens of a section (the tokens of one device), no expert is named by more than 20 entries, and in every draw some block has an expert named exactly 20 times. `bwd_ids`: the 2 entries of a token name different experts. In each aligned block of 64 tokens of a section (the tokens of one device), no expert is named by more than 20 entries, and in every draw some block has an expert named exactly 20 times.
All inputs are finite; a program needn't handle non-finite values.
Results may differ from the reference program's by a relative error of at most 0.017.
Values may be sent and summed in bfloat16 or wider, within the bound.
No kernel may reach another device: no remote copies, remote signals or barrier semaphores. Data moves between devices by JAX's collectives and lax.ppermute only.
A program may use at most 64 MiB of HBM per device.

```python
import math
import jax
import jax.numpy as jnp
import numpy as np
from jax import lax

D = 2048
HID = 384
TOPK = 2
TOK_DEV = 64
EXPERTS = 8
CAP = 20
TOKENS = 8192
N_DP = 16
N_SECTION = 8
N_EXPERT = 8


def block_scale(stream_key, dims, pieces, least, high):
    factor_of, own = 1.0, jax.random.fold_in(stream_key, 6)
    for axis_at, parts in pieces:
        draws = jnp.exp(jax.random.uniform(jax.random.fold_in(own, axis_at), (parts,), jnp.float32, least / len(pieces), high / len(pieces)))
        factor_of = factor_of * jnp.repeat(draws, dims[axis_at] // parts).reshape([-1 if axis == axis_at else 1 for axis in range(len(dims))])
    return factor_of


def routed_block(own_key, own, number, rows, number_of, top, most, slope):
    sequence = jax.random.permutation(own_key, number_of)
    crowded, ordinary = load_shares(number_of, rows * top, most, slope, True), load_shares(number_of, rows * top, most, slope, False)
    places = jnp.arange(number_of)

    def named(tallies, rotation):
        used = int((tallies > 0).sum())
        fixed = max(1, used // 4)
        passed = fixed + (places - fixed + rotation * (used - fixed)) % max(1, number_of - fixed)
        return jnp.zeros((number_of,), jnp.int32).at[sequence[jnp.where(places < fixed, places, passed)]].set(jnp.asarray(tallies, jnp.int32))

    tallies = jnp.where(number % 4 == 0, named(crowded, number // 4), named(ordinary, number - number // 4 - 1))
    mixed = jax.random.permutation(jax.random.fold_in(own, 3), number_of)
    source_of, sink = mixed[0:number_of // 2 * 2:2], mixed[1:number_of // 2 * 2:2]
    slack = jnp.minimum(tallies[source_of] - 1, most - tallies[sink]) // 2
    slack = jnp.where((source_of == sequence[0]) | (sink == sequence[0]) | (tallies[sink] == 0), 0, jnp.maximum(slack, 0))
    passed = jax.random.randint(jax.random.fold_in(own, 4), (number_of // 2,), 0, 1 << 20) % (slack + 1)
    tallies = tallies.at[source_of].add(-passed).at[sink].add(passed)
    members = jnp.searchsorted(jnp.cumsum(tallies), jnp.arange(rows * top), side="right").astype(jnp.int32)
    table = members.reshape(top, rows).T
    table = table[jax.random.permutation(jax.random.fold_in(own, 1), rows)]
    rotation = jax.random.randint(jax.random.fold_in(own, 2), (rows, 1), 0, top)
    return jnp.take_along_axis(table, (jnp.arange(top)[None, :] + rotation) % top, axis=1)


def load_shares(amount, total, reach, lean, full):
    portions = [(1 << 20) // math.isqrt(rank ** lean) + 1 for rank in range(1, amount + 1)]
    largest = reach if full else min(reach, max(-(-total // amount), total * portions[0] // sum(portions)))
    least = 1 if total - largest >= amount - 1 else 0
    counts, surplus = [largest] + [least] * (amount - 1), total - largest - least * (amount - 1)
    while surplus > 0:
        free = [i for i in range(1, amount) if counts[i] < largest] or [i for i in range(1, amount) if counts[i] < reach]
        pool, remaining = sum([portions[i] for i in free]), surplus
        for i in free:
            more = min(reach - counts[i], max(1, remaining * portions[i] // pool), surplus)
            counts[i] = counts[i] + more
            surplus = surplus - more
    return np.array(counts)


def bell_draw(rng, extent, spread, most, pieces=(), kind=jnp.bfloat16):
    entries = spread * jax.random.normal(rng, extent, jnp.float32)
    if pieces:
        entries = entries * block_scale(rng, extent, pieces, -0.22, 0.18)
    return jnp.clip(entries, -most, most).astype(kind)


def setup_inputs(seed: int = 0) -> dict:
    streams_of = jax.random.split(jax.random.key(seed), 12)
    act_in = bell_draw(streams_of[0], (N_SECTION, TOKENS, D), 1.0, 6.0, ((0, 8), (1, 128)))
    saved_in = bell_draw(streams_of[1], (N_SECTION, TOKENS, D), 1.0, 6.0, ((0, 8), (1, 128)))
    grad_in = bell_draw(streams_of[2], (N_SECTION, TOKENS, D), 1.0, 6.0, ((0, 8), (1, 128)))
    fwd_ids_keys = jax.random.split(jax.random.fold_in(streams_of[3], 1), N_SECTION * TOKENS // TOK_DEV)
    fwd_ids_turns = jax.random.permutation(jax.random.fold_in(streams_of[3], 3), N_SECTION * TOKENS // TOK_DEV)
    fwd_ids = jax.vmap(lambda own, number: routed_block(jax.random.fold_in(streams_of[3], 2), own, number, TOK_DEV, EXPERTS, TOPK, CAP, 1))(fwd_ids_keys, fwd_ids_turns).reshape((N_SECTION, TOKENS, TOPK))
    bwd_ids_keys = jax.random.split(jax.random.fold_in(streams_of[4], 1), N_SECTION * TOKENS // TOK_DEV)
    bwd_ids_turns = jax.random.permutation(jax.random.fold_in(streams_of[4], 3), N_SECTION * TOKENS // TOK_DEV)
    bwd_ids = jax.vmap(lambda own, number: routed_block(jax.random.fold_in(streams_of[4], 2), own, number, TOK_DEV, EXPERTS, TOPK, CAP, 1))(bwd_ids_keys, bwd_ids_turns).reshape((N_SECTION, TOKENS, TOPK))
    fwd_gates = jnp.clip(jnp.exp(math.log(1.0) - 1.609438 * jax.random.uniform(streams_of[5], (N_SECTION, TOKENS, TOPK), jnp.float32) ** block_scale(streams_of[5], (N_SECTION, TOKENS, TOPK), ((0, 8), (1, 128)), -0.2, 0.2)), 0.2, 1.0)
    bwd_gates = jnp.clip(jnp.exp(math.log(1.0) - 1.609438 * jax.random.uniform(streams_of[6], (N_SECTION, TOKENS, TOPK), jnp.float32) ** block_scale(streams_of[6], (N_SECTION, TOKENS, TOPK), ((0, 8), (1, 128)), -0.2, 0.2)), 0.2, 1.0)
    norm_gain = jnp.clip(1.0 + 0.1 * jax.random.normal(streams_of[7], (N_SECTION, D), jnp.float32), 0.5, 1.5)
    w_gate = bell_draw(streams_of[8], (N_SECTION, EXPERTS, D, HID), D ** -0.5, 0.125, ((0, 8), (1, 8)))
    w_up = bell_draw(streams_of[9], (N_SECTION, EXPERTS, D, HID), D ** -0.5, 0.125, ((0, 8), (1, 8)))
    w_down = bell_draw(streams_of[10], (N_SECTION, EXPERTS, HID, D), HID ** -0.5, 0.3125, ((0, 8), (1, 8)))
    return {"act_in": act_in, "saved_in": saved_in, "grad_in": grad_in, "fwd_ids": fwd_ids, "bwd_ids": bwd_ids, "fwd_gates": fwd_gates, "bwd_gates": bwd_gates, "norm_gain": norm_gain, "w_gate": w_gate, "w_up": w_up, "w_down": w_down}


EPS = 1e-06

def rms_norm(rows, gain):
    wide = rows.astype(jnp.float32)
    factor = lax.rsqrt(lax.optimization_barrier(jnp.mean(wide * wide, axis=-1, keepdims=True)) + EPS)
    return wide * factor * gain

def slot_numbers(ids):
    blocks = ids.reshape(-1, TOK_DEV * TOPK)
    onehot = (blocks[:, :, None] == jnp.arange(EXPERTS, dtype=jnp.int32)[None, None, :]).astype(jnp.int32)
    before = jnp.cumsum(onehot, axis=1) - onehot
    return lax.optimization_barrier(jnp.sum(before * onehot, axis=2)).reshape(ids.shape).astype(jnp.int32)

def owners():
    return (jnp.arange(TOKENS, dtype=jnp.int32) // TOK_DEV)[:, None] + jnp.zeros((1, TOPK), jnp.int32)

def pack(values, ids, slots):
    empty = jnp.zeros((EXPERTS, N_DP * N_EXPERT, CAP, values.shape[-1]), values.dtype)
    return empty.at[ids, owners(), slots].set(values)

def unpack(packed, ids, slots):
    return packed[ids, owners(), slots]

def expert_forward(args):
    rows, w_g, w_u, w_d = args
    flat = rows.reshape(-1, rows.shape[-1])
    pre_gate = jnp.dot(flat, w_g, preferred_element_type=jnp.float32)
    pre_up = jnp.dot(flat, w_u, preferred_element_type=jnp.float32)
    hidden = (jax.nn.silu(pre_gate) * pre_up).astype(jnp.bfloat16)
    produced = jnp.dot(hidden, w_d, preferred_element_type=jnp.float32).astype(jnp.bfloat16)
    return produced.reshape(rows.shape)

def expert_backward(args):
    rows, grads, w_g, w_u, w_d = args
    flat = rows.reshape(-1, rows.shape[-1])
    flat_grad = grads.reshape(-1, grads.shape[-1])
    pre_gate = jnp.dot(flat, w_g, preferred_element_type=jnp.float32)
    pre_up = jnp.dot(flat, w_u, preferred_element_type=jnp.float32)
    sig = jax.nn.sigmoid(pre_gate)
    silu_gate = jax.nn.silu(pre_gate)
    hidden = (silu_gate * pre_up).astype(jnp.bfloat16)
    hidden_grad = jnp.dot(flat_grad, w_d.T, preferred_element_type=jnp.float32)
    gate_grad = (hidden_grad * pre_up * sig * (1.0 + pre_gate * (1.0 - sig))).astype(jnp.bfloat16)
    up_grad = (hidden_grad * silu_gate).astype(jnp.bfloat16)
    slot_grad = (jnp.dot(gate_grad, w_g.T, preferred_element_type=jnp.float32) + jnp.dot(up_grad, w_u.T, preferred_element_type=jnp.float32)).astype(jnp.bfloat16)

    def per_replica(matrix):
        return matrix.reshape(N_DP, -1, matrix.shape[-1]).astype(jnp.float32)
    inputs_r = per_replica(flat)
    part_gate = jnp.einsum('rnk,rnh->rkh', inputs_r, per_replica(gate_grad))
    part_up = jnp.einsum('rnk,rnh->rkh', inputs_r, per_replica(up_grad))
    part_down = jnp.einsum('rnk,rnh->rkh', per_replica(flat_grad), per_replica(hidden))
    partial_value = (jnp.concatenate([part_gate, part_up, part_down], axis=2) / N_DP).astype(jnp.bfloat16)
    total = lax.optimization_barrier(jnp.sum(partial_value.astype(jnp.float32), axis=0))
    return (slot_grad.reshape(rows.shape), total)

def reference(act_in, saved_in, grad_in, fwd_ids, bwd_ids, fwd_gates, bwd_gates, norm_gain, w_gate, w_up, w_down):
    layer_outs = []
    input_grads = []
    weight_list = []
    for section in range(N_SECTION):
        gain = norm_gain[section]
        here = act_in[section]
        normed = rms_norm(here, gain).astype(jnp.bfloat16)
        slots = slot_numbers(fwd_ids[section])
        packed = pack(jnp.broadcast_to(normed[:, None, :], (TOKENS, TOPK, D)), fwd_ids[section], slots)
        produced = lax.map(expert_forward, (packed, w_gate[section], w_up[section], w_down[section]))
        gathered = unpack(produced, fwd_ids[section], slots).astype(jnp.float32)
        layer_out = (here.astype(jnp.float32) + lax.optimization_barrier(jnp.sum(fwd_gates[section][:, :, None] * gathered, axis=1))).astype(jnp.bfloat16)
        layer_outs.append(layer_out)
        saved_wide = saved_in[section].astype(jnp.float32)
        normed_wide, pull_back = jax.vjp(lambda v: rms_norm(v, gain), saved_wide)
        normed_bwd = normed_wide.astype(jnp.bfloat16)
        upstream = grad_in[section].astype(jnp.float32)
        out_grad = (bwd_gates[section][:, :, None] * upstream[:, None, :]).astype(jnp.bfloat16)
        back_slots = slot_numbers(bwd_ids[section])
        packed_in = pack(jnp.broadcast_to(normed_bwd[:, None, :], (TOKENS, TOPK, D)), bwd_ids[section], back_slots)
        packed_grad = pack(out_grad, bwd_ids[section], back_slots)
        slot_grad, totals = lax.map(expert_backward, (packed_in, packed_grad, w_gate[section], w_up[section], w_down[section]))
        normed_grad = lax.optimization_barrier(jnp.sum(unpack(slot_grad, bwd_ids[section], back_slots).astype(jnp.float32), axis=1))
        input_grad = (upstream + pull_back(normed_grad)[0]).astype(jnp.bfloat16)
        input_grads.append(input_grad)
        weight_list.append(totals)
    act_out = jnp.roll(jnp.stack(layer_outs), 1, axis=0)
    grad_out = jnp.roll(jnp.stack(input_grads), -1, axis=0)
    return (act_out, grad_out, jnp.stack(weight_list))
```

```python
import functools

import jax
import jax.numpy as jnp
from jax import lax
from jax.experimental import pallas as pl
from jax.experimental.pallas import tpu as pltpu
from jax.sharding import PartitionSpec as P

EPS = 1e-06
NOWHERE = -1000.0
CHUNK = 512
CONTRACT_FIRST = (((0,), (0,)), ((), ()))
CONTRACT_LAST = (((1,), (1,)), ((), ()))
HBM = pl.BlockSpec(memory_space=pltpu.HBM)


def matmul(a, b, dims=(((1,), (0,)), ((), ()))):
    return lax.dot_general(a, b, dims, preferred_element_type=jnp.float32)


def slot_table(ids, experts):
    tokens = ids.shape[1]
    expert = lax.broadcasted_iota(jnp.int32, (experts, tokens), 0)
    picks = [ids[k : k + 1, :] == expert for k in range(ids.shape[0])]
    member = functools.reduce(jnp.logical_or, picks)
    source = lax.broadcasted_iota(jnp.int32, (tokens, tokens), 0)
    target = lax.broadcasted_iota(jnp.int32, (tokens, tokens), 1)
    earlier = jnp.where(source < target, 1.0, 0.0).astype(jnp.bfloat16)
    before = matmul(jnp.where(member, 1.0, 0.0).astype(jnp.bfloat16), earlier)
    return picks, member, before


def spread(table, block):
    return jnp.concatenate(
        [jnp.broadcast_to(table[e : e + 1, :], (block, table.shape[1])) for e in range(table.shape[0])],
        axis=0,
    )


def slot_of_row(experts, block, tokens):
    one = lax.broadcasted_iota(jnp.int32, (block, tokens), 0).astype(jnp.float32)
    return jnp.concatenate([one] * experts, axis=0)


def onehot(mask):
    return jnp.where(mask, 1.0, 0.0).astype(jnp.bfloat16)


def start_all(pairs, sems):
    copies = [
        pltpu.make_async_copy(source, target, sems.at[i]) for i, (source, target) in enumerate(pairs)
    ]
    for copy in copies:
        copy.start()
    return copies


def wait_all(copies):
    for copy in copies:
        copy.wait()


def store_columns(stores, source, target, at, width, sems):
    cols = pl.ds(at, width)
    copy = pltpu.make_async_copy(source.at[:, cols], target.at[:, cols], sems.at[len(stores)])
    copy.start()
    stores.append(copy)


def row_factor(ref):
    width = ref.shape[1]
    total = jnp.zeros((ref.shape[0], 1), jnp.float32)
    for at in range(0, width, CHUNK):
        part = ref[:, at : at + CHUNK].astype(jnp.float32)
        total = total + jnp.sum(part * part, axis=1, keepdims=True)
    return lax.rsqrt(total / width + EPS)


def pack_bwd(experts, cap, ids_hbm, gates_hbm, saved_hbm, grad_hbm, gain_hbm, out_hbm, ids_ref, gates_ref, saved_ref, grad_ref, gain_ref, out_ref, sems, out_sems):
    copies = start_all(
        [
            (ids_hbm, ids_ref),
            (gates_hbm, gates_ref),
            (saved_hbm, saved_ref),
            (gain_hbm, gain_ref),
            (grad_hbm, grad_ref),
        ],
        sems,
    )
    wait_all(copies[:2])
    ids = ids_ref[...]
    tokens = ids.shape[1]
    block = 2 * cap
    picks, member, before = slot_table(ids, experts)
    rows = spread(jnp.where(member, before, NOWHERE), block)
    slot = slot_of_row(experts, block, tokens)
    hit_x = rows == slot
    hit_g = rows + cap == slot
    gate = spread(jnp.where(picks[0], gates_ref[0:1, :], gates_ref[1:2, :]), block)
    scale = jnp.sum(
        jnp.where(hit_x, 1.0, 0.0) + jnp.where(hit_g, gate, 0.0), axis=1, keepdims=True
    )
    place_x, place_g = onehot(hit_x), onehot(hit_g)
    wait_all(copies[2:])
    factor = row_factor(saved_ref)
    stores = []
    for at in range(0, saved_ref.shape[1], CHUNK):
        cols = slice(at, at + CHUNK)
        normed = (saved_ref[:, cols].astype(jnp.float32) * factor * gain_ref[:, cols]).astype(
            jnp.bfloat16
        )
        placed = matmul(place_x, normed) + matmul(place_g, grad_ref[:, cols])
        out_ref[:, cols] = (placed * scale).astype(jnp.bfloat16)
        store_columns(stores, out_ref, out_hbm, at, CHUNK, out_sems)
    wait_all(stores)


def pack_fwd(experts, cap, ids_hbm, act_hbm, gain_hbm, out_hbm, ids_ref, act_ref, gain_ref, out_ref, sems, out_sems):
    copies = start_all([(ids_hbm, ids_ref), (act_hbm, act_ref), (gain_hbm, gain_ref)], sems)
    wait_all(copies)
    ids = ids_ref[...]
    tokens = ids.shape[1]
    block = 2 * cap
    half = act_ref.shape[1] // 2
    _, member, before = slot_table(ids, experts)
    rows = spread(jnp.where(member, before, NOWHERE), block)
    slot = slot_of_row(experts, block, tokens)
    place_low, place_high = onehot(rows == slot), onehot(rows + cap == slot)
    factor = row_factor(act_ref)
    stores = []
    for at in range(0, half, CHUNK):
        low, high = slice(at, at + CHUNK), slice(half + at, half + at + CHUNK)
        normed_low = (act_ref[:, low].astype(jnp.float32) * factor * gain_ref[:, low]).astype(
            jnp.bfloat16
        )
        normed_high = (act_ref[:, high].astype(jnp.float32) * factor * gain_ref[:, high]).astype(
            jnp.bfloat16
        )
        out_ref[:, low] = (
            matmul(place_low, normed_low) + matmul(place_high, normed_high)
        ).astype(jnp.bfloat16)
        store_columns(stores, out_ref, out_hbm, at, CHUNK, out_sems)
    wait_all(stores)


def first_rows(shape, cap):
    row = lax.broadcasted_iota(jnp.int32, shape, 0)
    return lax.rem(row, 2 * cap) < cap


def expert_bwd(cap, scale, recv_hbm, gate_hbm, up_hbm, down_hbm, right_hbm, partial_hbm, recv_ref, right_ref, gate_ref, up_ref, down_ref, pre_g, pre_u, grad, out_ref, sems, out_sems):
    hid = gate_ref.shape[1]
    slots = recv_ref.shape[0]
    copies = start_all(
        [
            (recv_hbm, recv_ref),
            (down_hbm, down_ref),
            (gate_hbm, gate_ref),
            (up_hbm, up_ref),
        ],
        sems,
    )
    wait_all(copies[:2])
    grad[...] = matmul(recv_ref[...], down_ref[...], CONTRACT_LAST)
    copies[2].wait()
    pre_g[...] = matmul(recv_ref[...], gate_ref[...])
    copies[3].wait()
    pre_u[...] = matmul(recv_ref[...], up_ref[...])
    for at in range(0, hid, 128):
        cols = slice(at, at + 128)
        gate, up = pre_g[:, cols], pre_u[:, cols]
        hidden_grad = pltpu.roll(grad[:, cols], slots - cap, 0)
        first = first_rows(gate.shape, cap)
        sig = 1.0 / (1.0 + jnp.exp(-gate))
        silu = gate * sig
        zero = jnp.zeros_like(gate)
        gate_grad = hidden_grad * up * sig * (1.0 + gate * (1.0 - sig))
        right_ref[:, at : at + 128] = jnp.where(first, gate_grad, zero).astype(jnp.bfloat16)
        right_ref[:, hid + at : hid + at + 128] = jnp.where(
            first, hidden_grad * silu, zero
        ).astype(jnp.bfloat16)
        hidden = pltpu.roll(jnp.where(first, silu * up, zero), cap, 0)
        right_ref[:, 2 * hid + at : 2 * hid + at + 128] = hidden.astype(jnp.bfloat16)
    kept = pltpu.make_async_copy(right_ref, right_hbm, out_sems.at[2])
    kept.start()
    rows = out_ref.shape[1]
    stores = []
    for i in range(partial_hbm.shape[0] // rows):
        slot = i % 2
        if i >= 2:
            stores[i - 2].wait()
        left = recv_ref[:, i * rows : (i + 1) * rows]
        out_ref[slot] = (matmul(left, right_ref[...], CONTRACT_FIRST) * scale).astype(jnp.bfloat16)
        store = pltpu.make_async_copy(
            out_ref.at[slot], partial_hbm.at[pl.ds(i * rows, rows), :], out_sems.at[slot]
        )
        store.start()
        stores.append(store)
    wait_all(stores[-2:] + [kept])


def expert_fwd(cap, recv_hbm, right_hbm, gate_hbm, up_hbm, down_hbm, out_hbm, recv_ref, right_ref, out_ref, gate_ref, up_ref, down_ref, low_g, low_u, high_g, high_u, hid_ref, sems, out_sems):
    hid = gate_ref.shape[1]
    slots, half = recv_ref.shape
    copies = start_all(
        [
            (recv_hbm, recv_ref),
            (gate_hbm, gate_ref),
            (up_hbm, up_ref),
            (right_hbm, right_ref),
            (down_hbm, down_ref),
        ],
        sems,
    )
    wait_all(copies[:2])
    low_g[...] = matmul(recv_ref[...], gate_ref[:half, :])
    high_g[...] = matmul(recv_ref[...], gate_ref[half:, :])
    copies[2].wait()
    low_u[...] = matmul(recv_ref[...], up_ref[:half, :])
    high_u[...] = matmul(recv_ref[...], up_ref[half:, :])
    for at in range(0, hid, 128):
        cols = slice(at, at + 128)
        gate = low_g[:, cols] + pltpu.roll(high_g[:, cols], slots - cap, 0)
        up = low_u[:, cols] + pltpu.roll(high_u[:, cols], slots - cap, 0)
        hidden = gate / (1.0 + jnp.exp(-gate)) * up
        hidden = jnp.where(first_rows(gate.shape, cap), hidden, jnp.zeros_like(hidden))
        hid_ref[:, cols] = pltpu.roll(hidden, cap, 0).astype(jnp.bfloat16)
    wait_all(copies[3:])
    stores = []
    for at in range(0, out_ref.shape[1], CHUNK):
        cols = slice(at, at + CHUNK)
        total = matmul(hid_ref[...], down_ref[:, cols])
        total = total + matmul(right_ref[:, :hid], gate_ref[cols, :], CONTRACT_LAST)
        total = total + matmul(right_ref[:, hid : 2 * hid], up_ref[cols, :], CONTRACT_LAST)
        out_ref[:, cols] = total.astype(jnp.bfloat16)
        store_columns(stores, out_ref, out_hbm, at, CHUNK, out_sems)
    wait_all(stores)


def as_column(row):
    count = row.shape[1]
    down = lax.broadcasted_iota(jnp.int32, (count, count), 0)
    across = lax.broadcasted_iota(jnp.int32, (count, count), 1)
    kept = jnp.where(down == across, jnp.broadcast_to(row, (count, count)), 0.0)
    return jnp.sum(kept, axis=1, keepdims=True)


def combine(experts, cap, back_hbm, fwd_ids_hbm, bwd_ids_hbm, gates_hbm, act_hbm, saved_hbm, grad_hbm, gain_hbm, act_out_hbm, grad_out_hbm, act_out_ref, grad_out_ref, back_ref, fwd_ids_ref, bwd_ids_ref, gates_ref, act_ref, saved_ref, grad_ref, gain_ref, wide, sems, out_sems):
    copies = start_all(
        [
            (fwd_ids_hbm, fwd_ids_ref),
            (bwd_ids_hbm, bwd_ids_ref),
            (gates_hbm, gates_ref),
            (back_hbm, back_ref),
            (saved_hbm, saved_ref),
            (gain_hbm, gain_ref),
            (act_hbm, act_ref),
            (grad_hbm, grad_ref),
        ],
        sems,
    )
    wait_all(copies[:3])
    tokens, width = act_ref.shape
    block = 2 * cap
    slot = slot_of_row(experts, block, tokens)
    picks, _, before = slot_table(fwd_ids_ref[...], experts)
    chosen = [onehot(spread(jnp.where(pick, before, NOWHERE), block) + cap == slot) for pick in picks]
    gates = [as_column(gates_ref[k : k + 1, :]) for k in range(len(picks))]
    _, member, before = slot_table(bwd_ids_ref[...], experts)
    both = onehot(spread(jnp.where(member, before, NOWHERE), block) == slot)
    wait_all(copies[3:])
    factor = row_factor(saved_ref)
    inner = jnp.zeros((tokens, 1), jnp.float32)
    for at in range(0, width, CHUNK):
        cols = slice(at, at + CHUNK)
        back = back_ref[:, cols]
        total = gates[0] * matmul(chosen[0], back, CONTRACT_FIRST)
        total = total + gates[1] * matmul(chosen[1], back, CONTRACT_FIRST)
        act_out_ref[:, cols] = (act_ref[:, cols].astype(jnp.float32) + total).astype(jnp.bfloat16)
        scaled = matmul(both, back, CONTRACT_FIRST) * gain_ref[:, cols]
        wide[:, cols] = scaled
        inner = inner + jnp.sum(
            saved_ref[:, cols].astype(jnp.float32) * scaled, axis=1, keepdims=True
        )
    stores = []
    store_columns(stores, act_out_ref, act_out_hbm, 0, width, out_sems)
    pull = inner / width * factor * factor * factor
    for at in range(0, width, CHUNK):
        cols = slice(at, at + CHUNK)
        value = grad_ref[:, cols].astype(jnp.float32) + (
            wide[:, cols] * factor - saved_ref[:, cols].astype(jnp.float32) * pull
        )
        grad_out_ref[:, cols] = value.astype(jnp.bfloat16)
        store_columns(stores, grad_out_ref, grad_out_hbm, at, CHUNK, out_sems)
    wait_all(stores)


PARAMS = pltpu.CompilerParams(vmem_limit_bytes=66_800_000)


def cost(flops, moved):
    return pl.CostEstimate(flops=flops, bytes_accessed=moved, transcendentals=0)


def exchange(rows, experts):
    blocks = rows.reshape(experts, -1, rows.shape[-1])
    moved = lax.all_to_all(blocks, "expert", split_axis=0, concat_axis=0, tiled=True)
    return moved.reshape(rows.shape)


def shards(
    act_in,
    saved_in,
    grad_in,
    fwd_ids,
    bwd_ids,
    fwd_gates,
    bwd_gates,
    norm_gain,
    w_gate,
    w_up,
    w_down,
):
    experts = lax.axis_size("expert")
    replicas = lax.axis_size("dp")
    sections = lax.axis_size("section")
    tokens, width = act_in.shape[1:]
    topk = fwd_ids.shape[2]
    cap = min(tokens, 5 * tokens * topk // (4 * experts))
    slots = 2 * cap * experts
    here, saved, upstream = act_in[0], saved_in[0], grad_in[0]
    weight_gate, weight_up, weight_down = w_gate[0, 0], w_up[0, 0], w_down[0, 0]
    hid = weight_gate.shape[1]
    ids_fwd, ids_bwd = fwd_ids[0].T, bwd_ids[0].T
    gates_fwd, gates_bwd = fwd_gates[0].T, bwd_gates[0].T
    small = tokens * width * 2
    big = slots * width * 2
    weight_bytes = 3 * width * hid * 2
    ids_buf = pltpu.VMEM((topk, tokens), jnp.int32)
    gates_buf = pltpu.VMEM((topk, tokens), jnp.float32)
    rows_buf = pltpu.VMEM((tokens, width), jnp.bfloat16)
    gain_buf = pltpu.VMEM((1, width), jnp.float32)
    slots_buf = pltpu.VMEM((slots, width), jnp.bfloat16)
    half_buf = pltpu.VMEM((slots, width // 2), jnp.bfloat16)
    right_buf = pltpu.VMEM((slots, 3 * hid), jnp.bfloat16)
    chunks = width // CHUNK
    dma = lambda count: pltpu.SemaphoreType.DMA((count,))
    weight_bufs = [
        pltpu.VMEM((width, hid), jnp.bfloat16),
        pltpu.VMEM((width, hid), jnp.bfloat16),
        pltpu.VMEM((hid, width), jnp.bfloat16),
    ]

    send_bwd = pl.pallas_call(
        functools.partial(pack_bwd, experts, cap),
        out_shape=jax.ShapeDtypeStruct((slots, width), jnp.bfloat16),
        in_specs=[HBM] * 5,
        out_specs=HBM,
        scratch_shapes=[ids_buf, gates_buf, rows_buf, rows_buf, gain_buf, slots_buf, dma(5), dma(chunks)],
        compiler_params=PARAMS,
        cost_estimate=cost(4 * slots * tokens * width, 2 * small + big),
        name="pack_bwd",
    )(ids_bwd, gates_bwd, saved, upstream, norm_gain)
    recv_bwd = exchange(send_bwd, experts)
    send_fwd = pl.pallas_call(
        functools.partial(pack_fwd, experts, cap),
        out_shape=jax.ShapeDtypeStruct((slots, width // 2), jnp.bfloat16),
        in_specs=[HBM] * 3,
        out_specs=HBM,
        scratch_shapes=[ids_buf, rows_buf, gain_buf, half_buf, dma(3), dma(chunks)],
        compiler_params=PARAMS,
        cost_estimate=cost(2 * slots * tokens * width, small + big // 2),
        name="pack_fwd",
    )(ids_fwd, here, norm_gain)
    send_fwd, recv_bwd = lax.optimization_barrier((send_fwd, recv_bwd))
    recv_fwd = exchange(send_fwd, experts)

    right, partial = pl.pallas_call(
        functools.partial(expert_bwd, cap, 1.0 / replicas),
        out_shape=(
            jax.ShapeDtypeStruct((slots, 3 * hid), jnp.bfloat16),
            jax.ShapeDtypeStruct((width, 3 * hid), jnp.bfloat16),
        ),
        in_specs=[HBM] * 4,
        out_specs=(HBM, HBM),
        scratch_shapes=[slots_buf, right_buf]
        + weight_bufs
        + [pltpu.VMEM((slots, hid), jnp.float32)] * 3
        + [
            pltpu.VMEM((2, 256, 3 * hid), jnp.bfloat16),
            dma(4),
            dma(3),
        ],
        compiler_params=PARAMS,
        cost_estimate=cost(12 * slots * width * hid, big + 2 * weight_bytes),
        name="expert_bwd",
    )(recv_bwd, weight_gate, weight_up, weight_down)
    summed = lax.psum_scatter(partial, "dp", scatter_dimension=0, tiled=True)

    back = pl.pallas_call(
        functools.partial(expert_fwd, cap),
        out_shape=jax.ShapeDtypeStruct((slots, width), jnp.bfloat16),
        in_specs=[HBM] * 5,
        out_specs=HBM,
        scratch_shapes=[half_buf, right_buf, slots_buf]
        + weight_bufs
        + [pltpu.VMEM((slots, hid), jnp.float32)] * 4
        + [pltpu.VMEM((slots, hid), jnp.bfloat16), dma(5), dma(chunks)],
        compiler_params=PARAMS,
        cost_estimate=cost(10 * slots * width * hid, 2 * big + weight_bytes),
        name="expert_fwd",
    )(recv_fwd, right, weight_gate, weight_up, weight_down)
    returned = exchange(back, experts)

    layer_out, input_grad = pl.pallas_call(
        functools.partial(combine, experts, cap),
        out_shape=(
            jax.ShapeDtypeStruct((tokens, width), jnp.bfloat16),
            jax.ShapeDtypeStruct((tokens, width), jnp.bfloat16),
        ),
        in_specs=[HBM] * 8,
        out_specs=(HBM, HBM),
        scratch_shapes=[rows_buf, rows_buf, slots_buf, ids_buf, ids_buf, gates_buf, rows_buf, rows_buf, rows_buf, gain_buf]
        + [pltpu.VMEM((tokens, width), jnp.float32), dma(8), dma(chunks + 1)],
        compiler_params=PARAMS,
        cost_estimate=cost(6 * slots * tokens * width, big + 5 * small),
        name="combine",
    )(returned, ids_fwd, ids_bwd, gates_fwd, here, saved, upstream, norm_gain)
    ring = [(i, (i + 1) % sections) for i in range(sections)]
    act_out = lax.ppermute(layer_out, "section", ring)
    grad_out = lax.ppermute(input_grad, "section", [(target, source) for source, target in ring])
    return (act_out[None], grad_out[None], summed.astype(jnp.float32)[None, None])


def solution(mesh):
    tokens = P("section", ("dp", "expert"), None)
    weights = P("section", "expert", None, None)
    in_specs = (tokens,) * 7 + (P("section", None),) + (weights,) * 3
    out_specs = (tokens, tokens, P("section", "expert", "dp", None))

    return jax.shard_map(shards, mesh=mesh, in_specs=in_specs, out_specs=out_specs, check_vma=False)
```

```python
import functools

import jax
import jax.numpy as jnp
from jax import lax
from jax.experimental import pallas as pl
from jax.experimental.pallas import tpu as pltpu
from jax.sharding import PartitionSpec as P

EPS = 1e-06
NOWHERE = -1000.0
CHUNK = 512
CONTRACT_FIRST = (((0,), (0,)), ((), ()))
CONTRACT_LAST = (((1,), (1,)), ((), ()))
HBM = pl.BlockSpec(memory_space=pltpu.HBM)


def matmul(a, b, dims=(((1,), (0,)), ((), ()))):
    return lax.dot_general(a, b, dims, preferred_element_type=jnp.float32)


def slot_table(ids, experts):
    tokens = ids.shape[1]
    expert = lax.broadcasted_iota(jnp.int32, (experts, tokens), 0)
    picks = [ids[k : k + 1, :] == expert for k in range(ids.shape[0])]
    member = functools.reduce(jnp.logical_or, picks)
    source = lax.broadcasted_iota(jnp.int32, (tokens, tokens), 0)
    target = lax.broadcasted_iota(jnp.int32, (tokens, tokens), 1)
    earlier = jnp.where(source < target, 1.0, 0.0).astype(jnp.bfloat16)
    before = matmul(jnp.where(member, 1.0, 0.0).astype(jnp.bfloat16), earlier)
    return picks, member, before


def spread(table, block):
    return jnp.concatenate(
        [jnp.broadcast_to(table[e : e + 1, :], (block, table.shape[1])) for e in range(table.shape[0])],
        axis=0,
    )


def split(cap):
    main = cap // 8 * 8
    return main, cap - main


def slots_of_rows(experts, cap, tokens):
    main, tail = split(cap)
    row = lax.broadcasted_iota(jnp.int32, (2 * cap, tokens), 0)
    in_first = row < 2 * main + tail
    first = jnp.where(row < main, row, jnp.where((row >= 2 * main) & in_first, row - main, -1))
    second = jnp.where(
        (row >= main) & (row < 2 * main), row - main, jnp.where(in_first, -1, row - main - tail)
    )
    return [jnp.concatenate([one.astype(jnp.float32)] * experts, axis=0) for one in (first, second)]


def onehot(mask):
    return jnp.where(mask, 1.0, 0.0).astype(jnp.bfloat16)


def start_all(pairs, sems):
    copies = [
        pltpu.make_async_copy(source, target, sems.at[i]) for i, (source, target) in enumerate(pairs)
    ]
    for copy in copies:
        copy.start()
    return copies


def wait_all(copies):
    for copy in copies:
        copy.wait()


def store_columns(stores, source, target, at, width, sems):
    cols = pl.ds(at, width)
    copy = pltpu.make_async_copy(source.at[:, cols], target.at[:, cols], sems.at[len(stores)])
    copy.start()
    stores.append(copy)


def row_factor(ref):
    width = ref.shape[1]
    total = jnp.zeros((ref.shape[0], 1), jnp.float32)
    for at in range(0, width, CHUNK):
        part = ref[:, at : at + CHUNK].astype(jnp.float32)
        total = total + jnp.sum(part * part, axis=1, keepdims=True)
    return lax.rsqrt(total / width + EPS)


def pack_bwd(experts, cap, ids_hbm, gates_hbm, saved_hbm, grad_hbm, gain_hbm, out_hbm, ids_ref, gates_ref, saved_ref, grad_ref, gain_ref, out_ref, sems, out_sems):
    copies = start_all(
        [
            (ids_hbm, ids_ref),
            (gates_hbm, gates_ref),
            (saved_hbm, saved_ref),
            (gain_hbm, gain_ref),
            (grad_hbm, grad_ref),
        ],
        sems,
    )
    wait_all(copies[:2])
    ids = ids_ref[...]
    tokens = ids.shape[1]
    block = 2 * cap
    picks, member, before = slot_table(ids, experts)
    rows = spread(jnp.where(member, before, NOWHERE), block)
    first, second = slots_of_rows(experts, cap, tokens)
    hit_x, hit_g = rows == first, rows == second
    gate = spread(jnp.where(picks[0], gates_ref[0:1, :], gates_ref[1:2, :]), block)
    scale = jnp.sum(
        jnp.where(hit_x, 1.0, 0.0) + jnp.where(hit_g, gate, 0.0), axis=1, keepdims=True
    )
    place_x, place_g = onehot(hit_x), onehot(hit_g)
    wait_all(copies[2:])
    factor = row_factor(saved_ref)
    stores = []
    for at in range(0, saved_ref.shape[1], CHUNK):
        cols = slice(at, at + CHUNK)
        normed = (saved_ref[:, cols].astype(jnp.float32) * factor * gain_ref[:, cols]).astype(
            jnp.bfloat16
        )
        placed = matmul(place_x, normed) + matmul(place_g, grad_ref[:, cols])
        out_ref[:, cols] = (placed * scale).astype(jnp.bfloat16)
        store_columns(stores, out_ref, out_hbm, at, CHUNK, out_sems)
    wait_all(stores)


def pack_fwd(experts, cap, ids_hbm, act_hbm, gain_hbm, out_hbm, ids_ref, act_ref, gain_ref, out_ref, sems, out_sems):
    copies = start_all([(ids_hbm, ids_ref), (act_hbm, act_ref), (gain_hbm, gain_ref)], sems)
    wait_all(copies)
    ids = ids_ref[...]
    tokens = ids.shape[1]
    block = 2 * cap
    half = act_ref.shape[1] // 2
    _, member, before = slot_table(ids, experts)
    rows = spread(jnp.where(member, before, NOWHERE), block)
    first, second = slots_of_rows(experts, cap, tokens)
    place_low, place_high = onehot(rows == first), onehot(rows == second)
    factor = row_factor(act_ref)
    stores = []
    for at in range(0, half, CHUNK):
        low, high = slice(at, at + CHUNK), slice(half + at, half + at + CHUNK)
        normed_low = (act_ref[:, low].astype(jnp.float32) * factor * gain_ref[:, low]).astype(
            jnp.bfloat16
        )
        normed_high = (act_ref[:, high].astype(jnp.float32) * factor * gain_ref[:, high]).astype(
            jnp.bfloat16
        )
        out_ref[:, low] = (
            matmul(place_low, normed_low) + matmul(place_high, normed_high)
        ).astype(jnp.bfloat16)
        store_columns(stores, out_ref, out_hbm, at, CHUNK, out_sems)
    wait_all(stores)


def sorted_rows(blocks, cap):
    main, tail = split(cap)
    block, whole, short = 2 * cap, blocks * main, 2 * tail
    firsts = [(pl.ds(i * block, main), pl.ds(i * main, main)) for i in range(blocks)]
    seconds = [(pl.ds(i * block + main, main), pl.ds(i * main, main)) for i in range(blocks)]
    tails = [
        (pl.ds(i * block + 2 * main, short), pl.ds(whole + i * short, short)) for i in range(blocks)
    ]
    return firsts, seconds, tails


def first_rows(shape, whole, tail):
    row = lax.broadcasted_iota(jnp.int32, shape, 0)
    return (row < whole) | (lax.rem(row - whole + 2 * tail, 2 * tail) < tail)


def shift_tail(value, whole, by):
    short = value.shape[0] - whole
    return jnp.concatenate([value[:whole], pltpu.roll(value[whole:], by % short, 0)], axis=0)


def expert_bwd(blocks, cap, scale, recv_hbm, gate_hbm, up_hbm, down_hbm, right_hbm, partial_hbm, x_ref, g_ref, right_ref, hid_ref, gate_ref, up_ref, down_ref, pre_g, pre_u, grad, out_ref, sems, out_sems):
    hid = gate_ref.shape[1]
    main, tail = split(cap)
    whole = blocks * main
    firsts, seconds, tails = sorted_rows(blocks, cap)
    copies = start_all(
        [(recv_hbm.at[source, :], g_ref.at[target, :]) for source, target in seconds + tails]
        + [(down_hbm, down_ref)]
        + [(recv_hbm.at[source, :], x_ref.at[target, :]) for source, target in firsts + tails]
        + [(gate_hbm, gate_ref), (up_hbm, up_ref)],
        sems,
    )
    wait_all(copies[: 2 * blocks + 1])
    grad[...] = matmul(g_ref[...], down_ref[...], CONTRACT_LAST)
    wait_all(copies[2 * blocks + 1 : 4 * blocks + 2])
    pre_g[...] = matmul(x_ref[...], gate_ref[...])
    wait_all(copies[4 * blocks + 2 :])
    pre_u[...] = matmul(x_ref[...], up_ref[...])
    for at in range(0, hid, 128):
        cols = slice(at, at + 128)
        gate, up = pre_g[:, cols], pre_u[:, cols]
        hidden_grad = shift_tail(grad[:, cols], whole, -tail)
        first = first_rows(gate.shape, whole, tail)
        sig = 1.0 / (1.0 + jnp.exp(-gate))
        silu = gate * sig
        zero = jnp.zeros_like(gate)
        gate_grad = hidden_grad * up * sig * (1.0 + gate * (1.0 - sig))
        right_ref[:, at : at + 128] = jnp.where(first, gate_grad, zero).astype(jnp.bfloat16)
        right_ref[:, hid + at : hid + at + 128] = jnp.where(
            first, hidden_grad * silu, zero
        ).astype(jnp.bfloat16)
        hidden = shift_tail(jnp.where(first, silu * up, zero), whole, tail)
        hid_ref[:, cols] = hidden.astype(jnp.bfloat16)
    kept = pltpu.make_async_copy(right_ref, right_hbm, out_sems.at[2])
    kept.start()
    rows = out_ref.shape[1]
    stores = []
    for i in range(partial_hbm.shape[0] // rows):
        slot = i % 2
        if i >= 2:
            stores[i - 2].wait()
        span = slice(i * rows, (i + 1) * rows)
        wide = matmul(x_ref[:, span], right_ref[...], CONTRACT_FIRST) * scale
        out_ref[slot, :, : 2 * hid] = wide.astype(jnp.bfloat16)
        wide = matmul(g_ref[:, span], hid_ref[...], CONTRACT_FIRST) * scale
        out_ref[slot, :, 2 * hid :] = wide.astype(jnp.bfloat16)
        store = pltpu.make_async_copy(
            out_ref.at[slot], partial_hbm.at[pl.ds(i * rows, rows), :], out_sems.at[slot]
        )
        store.start()
        stores.append(store)
    wait_all(stores[-2:] + [kept])


def expert_fwd(blocks, cap, recv_hbm, right_hbm, gate_hbm, up_hbm, down_hbm, out_hbm, rows_ref, right_ref, one_ref, two_ref, gate_ref, up_ref, down_ref, low_g, low_u, high_g, high_u, hid_ref, sems, out_sems):
    hid = gate_ref.shape[1]
    main, tail = split(cap)
    whole = blocks * main
    half = recv_hbm.shape[1]
    firsts, seconds, tails = sorted_rows(blocks, cap)
    low_cols, high_cols = pl.ds(0, half), pl.ds(half, half)
    copies = start_all(
        [(recv_hbm.at[source, :], rows_ref.at[target, low_cols]) for source, target in firsts + tails]
        + [(recv_hbm.at[source, :], rows_ref.at[target, high_cols]) for source, target in seconds + tails]
        + [(gate_hbm, gate_ref), (up_hbm, up_ref), (right_hbm, right_ref), (down_hbm, down_ref)],
        sems,
    )
    wait_all(copies[:-3])
    low_g[...] = matmul(rows_ref[:, :half], gate_ref[:half, :])
    high_g[...] = matmul(rows_ref[:, half:], gate_ref[half:, :])
    copies[-3].wait()
    low_u[...] = matmul(rows_ref[:, :half], up_ref[:half, :])
    high_u[...] = matmul(rows_ref[:, half:], up_ref[half:, :])
    for at in range(0, hid, 128):
        cols = slice(at, at + 128)
        gate = low_g[:, cols] + shift_tail(high_g[:, cols], whole, -tail)
        up = low_u[:, cols] + shift_tail(high_u[:, cols], whole, -tail)
        hidden = gate / (1.0 + jnp.exp(-gate)) * up
        hidden = jnp.where(first_rows(gate.shape, whole, tail), hidden, jnp.zeros_like(hidden))
        hid_ref[:, cols] = shift_tail(hidden, whole, tail).astype(jnp.bfloat16)
    wait_all(copies[-2:])
    stores = []
    width = out_hbm.shape[1]
    span = width // 2
    for start in range(0, width, span):
        for at in range(start, start + span, CHUNK):
            cols = slice(at, at + CHUNK)
            one = matmul(right_ref[:, :hid], gate_ref[cols, :], CONTRACT_LAST)
            one = one + matmul(right_ref[:, hid:], up_ref[cols, :], CONTRACT_LAST)
            two = matmul(hid_ref[...], down_ref[:, cols])
            one_ref[:whole, cols] = one[:whole].astype(jnp.bfloat16)
            one_ref[whole:, cols] = (one[whole:] + two[whole:]).astype(jnp.bfloat16)
            two_ref[:, cols] = two[:whole].astype(jnp.bfloat16)
        part = pl.ds(start, span)
        for source, targets in ((one_ref, firsts), (two_ref, seconds), (one_ref, tails)):
            for target, rows in targets:
                copy = pltpu.make_async_copy(
                    source.at[rows, part], out_hbm.at[target, part], out_sems.at[len(stores)]
                )
                copy.start()
                stores.append(copy)
    wait_all(stores)


def widen(narrow_hbm, wide_hbm, narrow_ref, wide_ref, sems):
    parts = narrow_ref.shape[0] // 32
    spans = [pl.ds(i * 32, 32) for i in range(parts)]
    copies = start_all([(narrow_hbm.at[span, :], narrow_ref.at[span, :]) for span in spans], sems)
    stores = []
    for i, span in enumerate(spans):
        copies[i].wait()
        wide_ref[span, :] = narrow_ref[span, :].astype(jnp.float32)
        store = pltpu.make_async_copy(wide_ref.at[span, :], wide_hbm.at[span, :], sems.at[parts + i])
        store.start()
        stores.append(store)
    wait_all(stores)


def settle(one_hbm, two_hbm, one_out, two_out, one_ref, two_ref, sems):
    copies = start_all([(one_hbm, one_ref), (two_hbm, two_ref)], sems)
    stores = []
    for i, (held, target) in enumerate(((one_ref, one_out), (two_ref, two_out))):
        copies[i].wait()
        store = pltpu.make_async_copy(held, target, sems.at[2 + i])
        store.start()
        stores.append(store)
    wait_all(stores)


def as_column(row):
    count = row.shape[1]
    down = lax.broadcasted_iota(jnp.int32, (count, count), 0)
    across = lax.broadcasted_iota(jnp.int32, (count, count), 1)
    kept = jnp.where(down == across, jnp.broadcast_to(row, (count, count)), 0.0)
    return jnp.sum(kept, axis=1, keepdims=True)


def combine(experts, cap, back_hbm, fwd_ids_hbm, bwd_ids_hbm, gates_hbm, act_hbm, saved_hbm, grad_hbm, gain_hbm, act_out_hbm, grad_out_hbm, act_out_ref, grad_out_ref, back_ref, fwd_ids_ref, bwd_ids_ref, gates_ref, act_ref, saved_ref, grad_ref, gain_ref, wide, sems, out_sems):
    copies = start_all(
        [
            (fwd_ids_hbm, fwd_ids_ref),
            (bwd_ids_hbm, bwd_ids_ref),
            (gates_hbm, gates_ref),
            (back_hbm, back_ref),
            (saved_hbm, saved_ref),
            (gain_hbm, gain_ref),
            (act_hbm, act_ref),
            (grad_hbm, grad_ref),
        ],
        sems,
    )
    wait_all(copies[:3])
    tokens, width = act_ref.shape
    block = 2 * cap
    first, second = slots_of_rows(experts, cap, tokens)
    picks, _, before = slot_table(fwd_ids_ref[...], experts)
    chosen = [onehot(spread(jnp.where(pick, before, NOWHERE), block) == second) for pick in picks]
    gates = [as_column(gates_ref[k : k + 1, :]) for k in range(len(picks))]
    _, member, before = slot_table(bwd_ids_ref[...], experts)
    both = onehot(spread(jnp.where(member, before, NOWHERE), block) == first)
    wait_all(copies[3:])
    factor = row_factor(saved_ref)
    inner = jnp.zeros((tokens, 1), jnp.float32)
    for at in range(0, width, CHUNK):
        cols = slice(at, at + CHUNK)
        back = back_ref[:, cols]
        total = gates[0] * matmul(chosen[0], back, CONTRACT_FIRST)
        total = total + gates[1] * matmul(chosen[1], back, CONTRACT_FIRST)
        act_out_ref[:, cols] = (act_ref[:, cols].astype(jnp.float32) + total).astype(jnp.bfloat16)
        scaled = matmul(both, back, CONTRACT_FIRST) * gain_ref[:, cols]
        wide[:, cols] = scaled
        inner = inner + jnp.sum(
            saved_ref[:, cols].astype(jnp.float32) * scaled, axis=1, keepdims=True
        )
    stores = []
    store_columns(stores, act_out_ref, act_out_hbm, 0, width, out_sems)
    pull = inner / width * factor * factor * factor
    for at in range(0, width, CHUNK):
        cols = slice(at, at + CHUNK)
        value = grad_ref[:, cols].astype(jnp.float32) + (
            wide[:, cols] * factor - saved_ref[:, cols].astype(jnp.float32) * pull
        )
        grad_out_ref[:, cols] = value.astype(jnp.bfloat16)
        store_columns(stores, grad_out_ref, grad_out_hbm, at, CHUNK, out_sems)
    wait_all(stores)


PARAMS = pltpu.CompilerParams(vmem_limit_bytes=66_800_000)


def cost(flops, moved):
    return pl.CostEstimate(flops=flops, bytes_accessed=moved, transcendentals=0)


def exchange(rows, experts):
    blocks = rows.reshape(experts, -1, rows.shape[-1])
    moved = lax.all_to_all(blocks, "expert", split_axis=0, concat_axis=0, tiled=True)
    return moved.reshape(rows.shape)


def shards(
    act_in,
    saved_in,
    grad_in,
    fwd_ids,
    bwd_ids,
    fwd_gates,
    bwd_gates,
    norm_gain,
    w_gate,
    w_up,
    w_down,
):
    experts = lax.axis_size("expert")
    replicas = lax.axis_size("dp")
    sections = lax.axis_size("section")
    tokens, width = act_in.shape[1:]
    topk = fwd_ids.shape[2]
    cap = min(tokens, 5 * tokens * topk // (4 * experts))
    slots = 2 * cap * experts
    here, saved, upstream = act_in[0], saved_in[0], grad_in[0]
    weight_gate, weight_up, weight_down = w_gate[0, 0], w_up[0, 0], w_down[0, 0]
    hid = weight_gate.shape[1]
    ids_fwd, ids_bwd = fwd_ids[0].T, bwd_ids[0].T
    gates_fwd, gates_bwd = fwd_gates[0].T, bwd_gates[0].T
    small = tokens * width * 2
    big = slots * width * 2
    weight_bytes = 3 * width * hid * 2
    ids_buf = pltpu.VMEM((topk, tokens), jnp.int32)
    gates_buf = pltpu.VMEM((topk, tokens), jnp.float32)
    rows_buf = pltpu.VMEM((tokens, width), jnp.bfloat16)
    gain_buf = pltpu.VMEM((1, width), jnp.float32)
    slots_buf = pltpu.VMEM((slots, width), jnp.bfloat16)
    half_buf = pltpu.VMEM((slots, width // 2), jnp.bfloat16)
    main, tail = split(cap)
    rows = experts * (main + 2 * tail)
    sorted_buf = pltpu.VMEM((rows, width), jnp.bfloat16)
    right_buf = pltpu.VMEM((rows, 2 * hid), jnp.bfloat16)
    hid_buf = pltpu.VMEM((rows, hid), jnp.bfloat16)
    chunks = width // CHUNK
    dma = lambda count: pltpu.SemaphoreType.DMA((count,))
    weight_bufs = [
        pltpu.VMEM((width, hid), jnp.bfloat16),
        pltpu.VMEM((width, hid), jnp.bfloat16),
        pltpu.VMEM((hid, width), jnp.bfloat16),
    ]

    send_bwd = pl.pallas_call(
        functools.partial(pack_bwd, experts, cap),
        out_shape=jax.ShapeDtypeStruct((slots, width), jnp.bfloat16),
        in_specs=[HBM] * 5,
        out_specs=HBM,
        scratch_shapes=[ids_buf, gates_buf, rows_buf, rows_buf, gain_buf, slots_buf, dma(5), dma(chunks)],
        compiler_params=PARAMS,
        cost_estimate=cost(4 * slots * tokens * width, 2 * small + big),
        name="pack_bwd",
    )(ids_bwd, gates_bwd, saved, upstream, norm_gain)
    recv_bwd = exchange(send_bwd, experts)
    send_fwd = pl.pallas_call(
        functools.partial(pack_fwd, experts, cap),
        out_shape=jax.ShapeDtypeStruct((slots, width // 2), jnp.bfloat16),
        in_specs=[HBM] * 3,
        out_specs=HBM,
        scratch_shapes=[ids_buf, rows_buf, gain_buf, half_buf, dma(3), dma(chunks)],
        compiler_params=PARAMS,
        cost_estimate=cost(2 * slots * tokens * width, small + big // 2),
        name="pack_fwd",
    )(ids_fwd, here, norm_gain)

    right, partial = pl.pallas_call(
        functools.partial(expert_bwd, experts, cap, 1.0 / replicas),
        out_shape=(
            jax.ShapeDtypeStruct((rows, 2 * hid), jnp.bfloat16),
            jax.ShapeDtypeStruct((width, 3 * hid), jnp.bfloat16),
        ),
        in_specs=[HBM] * 4,
        out_specs=(HBM, HBM),
        scratch_shapes=[sorted_buf, sorted_buf, right_buf, hid_buf]
        + weight_bufs
        + [pltpu.VMEM((rows, hid), jnp.float32)] * 3
        + [
            pltpu.VMEM((2, 256, 3 * hid), jnp.bfloat16),
            dma(4 * experts + 3),
            dma(3),
        ],
        compiler_params=PARAMS,
        cost_estimate=cost(12 * slots * width * hid, big + 2 * weight_bytes),
        name="expert_bwd",
    )(recv_bwd, weight_gate, weight_up, weight_down)
    summed = lax.psum_scatter(partial, "dp", scatter_dimension=0, tiled=True)
    total = pl.pallas_call(
        widen,
        out_shape=jax.ShapeDtypeStruct(summed.shape, jnp.float32),
        in_specs=[HBM],
        out_specs=HBM,
        scratch_shapes=[
            pltpu.VMEM(summed.shape, jnp.bfloat16),
            pltpu.VMEM(summed.shape, jnp.float32),
            dma(2 * (summed.shape[0] // 32)),
        ],
        compiler_params=PARAMS,
        cost_estimate=cost(0, 6 * summed.size),
        name="widen",
    )(summed)

    send_fwd, right = lax.optimization_barrier((send_fwd, right))
    recv_fwd = exchange(send_fwd, experts)

    back = pl.pallas_call(
        functools.partial(expert_fwd, experts, cap),
        out_shape=jax.ShapeDtypeStruct((slots, width), jnp.bfloat16),
        in_specs=[HBM] * 5,
        out_specs=HBM,
        scratch_shapes=[sorted_buf, right_buf, sorted_buf, pltpu.VMEM((main * experts, width), jnp.bfloat16)]
        + weight_bufs
        + [pltpu.VMEM((rows, hid), jnp.float32)] * 4
        + [hid_buf, dma(4 * experts + 4), dma(6 * experts)],
        compiler_params=PARAMS,
        cost_estimate=cost(10 * slots * width * hid, 2 * big + weight_bytes),
        name="expert_fwd",
    )(recv_fwd, right, weight_gate, weight_up, weight_down)
    returned = exchange(back, experts)

    layer_out, input_grad = pl.pallas_call(
        functools.partial(combine, experts, cap),
        out_shape=(
            jax.ShapeDtypeStruct((tokens, width), jnp.bfloat16),
            jax.ShapeDtypeStruct((tokens, width), jnp.bfloat16),
        ),
        in_specs=[HBM] * 8,
        out_specs=(HBM, HBM),
        scratch_shapes=[rows_buf, rows_buf, slots_buf, ids_buf, ids_buf, gates_buf, rows_buf, rows_buf, rows_buf, gain_buf]
        + [pltpu.VMEM((tokens, width), jnp.float32), dma(8), dma(chunks + 1)],
        compiler_params=PARAMS,
        cost_estimate=cost(6 * slots * tokens * width, big + 5 * small),
        name="combine",
    )(returned, ids_fwd, ids_bwd, gates_fwd, here, saved, upstream, norm_gain)
    ring = [(i, (i + 1) % sections) for i in range(sections)]
    act_out = lax.ppermute(layer_out, "section", ring)
    grad_out = lax.ppermute(input_grad, "section", [(target, source) for source, target in ring])
    act_out, grad_out = pl.pallas_call(
        settle,
        out_shape=(
            jax.ShapeDtypeStruct(act_out.shape, act_out.dtype),
            jax.ShapeDtypeStruct(grad_out.shape, grad_out.dtype),
        ),
        in_specs=[HBM, HBM],
        out_specs=(HBM, HBM),
        scratch_shapes=[rows_buf, rows_buf, dma(4)],
        compiler_params=PARAMS,
        cost_estimate=cost(0, 4 * small),
        name="settle",
    )(act_out, grad_out)
    return (act_out[None], grad_out[None], total[None, None])


def solution(mesh):
    tokens = P("section", ("dp", "expert"), None)
    weights = P("section", "expert", None, None)
    in_specs = (tokens,) * 7 + (P("section", None),) + (weights,) * 3
    out_specs = (tokens, tokens, P("section", "expert", "dp", None))

    return jax.shard_map(shards, mesh=mesh, in_specs=in_specs, out_specs=out_specs, check_vma=False)
```

```python
import functools

import jax
import jax.numpy as jnp
from jax import lax
from jax.experimental import pallas as pl
from jax.experimental.pallas import tpu as pltpu
from jax.sharding import PartitionSpec as P

EPS = 1e-06
NOWHERE = -1000.0
CHUNK = 512
CONTRACT_FIRST = (((0,), (0,)), ((), ()))
CONTRACT_LAST = (((1,), (1,)), ((), ()))
HBM = pl.BlockSpec(memory_space=pltpu.HBM)


def matmul(a, b, dims=(((1,), (0,)), ((), ()))):
    return lax.dot_general(a, b, dims, preferred_element_type=jnp.float32)


def slot_table(ids, experts):
    tokens = ids.shape[1]
    expert = lax.broadcasted_iota(jnp.int32, (experts, tokens), 0)
    picks = [ids[k : k + 1, :] == expert for k in range(ids.shape[0])]
    member = functools.reduce(jnp.logical_or, picks)
    source = lax.broadcasted_iota(jnp.int32, (tokens, tokens), 0)
    target = lax.broadcasted_iota(jnp.int32, (tokens, tokens), 1)
    earlier = jnp.where(source < target, 1.0, 0.0).astype(jnp.bfloat16)
    before = matmul(jnp.where(member, 1.0, 0.0).astype(jnp.bfloat16), earlier)
    return picks, member, before


def spread(table, block):
    return jnp.concatenate(
        [jnp.broadcast_to(table[e : e + 1, :], (block, table.shape[1])) for e in range(table.shape[0])],
        axis=0,
    )


def split(cap):
    main = cap // 8 * 8
    return main, cap - main


def slots_of_rows(experts, cap, tokens):
    main, tail = split(cap)
    row = lax.broadcasted_iota(jnp.int32, (2 * cap, tokens), 0)
    in_first = row < 2 * main + tail
    first = jnp.where(row < main, row, jnp.where((row >= 2 * main) & in_first, row - main, -1))
    second = jnp.where(
        (row >= main) & (row < 2 * main), row - main, jnp.where(in_first, -1, row - main - tail)
    )
    return [jnp.concatenate([one.astype(jnp.float32)] * experts, axis=0) for one in (first, second)]


def onehot(mask):
    return jnp.where(mask, 1.0, 0.0).astype(jnp.bfloat16)


def start_all(pairs, sems):
    copies = [
        pltpu.make_async_copy(source, target, sems.at[i]) for i, (source, target) in enumerate(pairs)
    ]
    for copy in copies:
        copy.start()
    return copies


def wait_all(copies):
    for copy in copies:
        copy.wait()


def store_columns(stores, source, target, at, width, sems):
    cols = pl.ds(at, width)
    copy = pltpu.make_async_copy(source.at[:, cols], target.at[:, cols], sems.at[len(stores)])
    copy.start()
    stores.append(copy)


def row_factor(ref):
    width = ref.shape[1]
    total = jnp.zeros((ref.shape[0], 1), jnp.float32)
    for at in range(0, width, CHUNK):
        part = ref[:, at : at + CHUNK].astype(jnp.float32)
        total = total + jnp.sum(part * part, axis=1, keepdims=True)
    return lax.rsqrt(total / width + EPS)


def pack_bwd(experts, cap, ids_hbm, gates_hbm, saved_hbm, grad_hbm, gain_hbm, out_hbm, ids_ref, gates_ref, saved_ref, grad_ref, gain_ref, out_ref, sems, out_sems):
    copies = start_all(
        [
            (ids_hbm, ids_ref),
            (gates_hbm, gates_ref),
            (saved_hbm, saved_ref),
            (gain_hbm, gain_ref),
            (grad_hbm, grad_ref),
        ],
        sems,
    )
    wait_all(copies[:2])
    ids = ids_ref[...]
    tokens = ids.shape[1]
    block = 2 * cap
    picks, member, before = slot_table(ids, experts)
    rows = spread(jnp.where(member, before, NOWHERE), block)
    first, second = slots_of_rows(experts, cap, tokens)
    hit_x, hit_g = rows == first, rows == second
    gate = spread(jnp.where(picks[0], gates_ref[0:1, :], gates_ref[1:2, :]), block)
    scale = jnp.sum(
        jnp.where(hit_x, 1.0, 0.0) + jnp.where(hit_g, gate, 0.0), axis=1, keepdims=True
    )
    place_x, place_g = onehot(hit_x), onehot(hit_g)
    wait_all(copies[2:])
    factor = row_factor(saved_ref)
    stores = []
    for at in range(0, saved_ref.shape[1], CHUNK):
        cols = slice(at, at + CHUNK)
        normed = (saved_ref[:, cols].astype(jnp.float32) * factor * gain_ref[:, cols]).astype(
            jnp.bfloat16
        )
        placed = matmul(place_x, normed) + matmul(place_g, grad_ref[:, cols])
        out_ref[:, cols] = (placed * scale).astype(jnp.bfloat16)
        store_columns(stores, out_ref, out_hbm, at, CHUNK, out_sems)
    wait_all(stores)


def pack_fwd(experts, cap, ids_hbm, act_hbm, gain_hbm, out_hbm, ids_ref, act_ref, gain_ref, out_ref, sems, out_sems):
    copies = start_all([(ids_hbm, ids_ref), (act_hbm, act_ref), (gain_hbm, gain_ref)], sems)
    wait_all(copies)
    ids = ids_ref[...]
    tokens = ids.shape[1]
    block = 2 * cap
    half = act_ref.shape[1] // 2
    _, member, before = slot_table(ids, experts)
    rows = spread(jnp.where(member, before, NOWHERE), block)
    first, second = slots_of_rows(experts, cap, tokens)
    place_low, place_high = onehot(rows == first), onehot(rows == second)
    factor = row_factor(act_ref)
    stores = []
    for at in range(0, half, CHUNK):
        low, high = slice(at, at + CHUNK), slice(half + at, half + at + CHUNK)
        normed_low = (act_ref[:, low].astype(jnp.float32) * factor * gain_ref[:, low]).astype(
            jnp.bfloat16
        )
        normed_high = (act_ref[:, high].astype(jnp.float32) * factor * gain_ref[:, high]).astype(
            jnp.bfloat16
        )
        out_ref[:, low] = (
            matmul(place_low, normed_low) + matmul(place_high, normed_high)
        ).astype(jnp.bfloat16)
        store_columns(stores, out_ref, out_hbm, at, CHUNK, out_sems)
    wait_all(stores)


def sorted_rows(blocks, cap):
    main, tail = split(cap)
    block, whole, short = 2 * cap, blocks * main, 2 * tail
    firsts = [(pl.ds(i * block, main), pl.ds(i * main, main)) for i in range(blocks)]
    seconds = [(pl.ds(i * block + main, main), pl.ds(i * main, main)) for i in range(blocks)]
    tails = [
        (pl.ds(i * block + 2 * main, short), pl.ds(whole + i * short, short)) for i in range(blocks)
    ]
    return firsts, seconds, tails


def first_rows(shape, whole, tail):
    row = lax.broadcasted_iota(jnp.int32, shape, 0)
    return (row < whole) | (lax.rem(row - whole + 2 * tail, 2 * tail) < tail)


def shift_tail(value, whole, by):
    short = value.shape[0] - whole
    return jnp.concatenate([value[:whole], pltpu.roll(value[whole:], by % short, 0)], axis=0)


def expert_bwd(blocks, cap, scale, recv_hbm, gate_hbm, up_hbm, down_hbm, right_hbm, partial_hbm, x_ref, g_ref, right_ref, hid_ref, pair_ref, down_ref, pre, grad, out_ref, sems, out_sems):
    hid = down_ref.shape[0]
    main, tail = split(cap)
    whole = blocks * main
    firsts, seconds, tails = sorted_rows(blocks, cap)
    copies = start_all(
        [(recv_hbm.at[source, :], g_ref.at[target, :]) for source, target in seconds + tails]
        + [(down_hbm, down_ref)]
        + [(recv_hbm.at[source, :], x_ref.at[target, :]) for source, target in firsts + tails]
        + [(gate_hbm, pair_ref.at[:, pl.ds(0, hid)]), (up_hbm, pair_ref.at[:, pl.ds(hid, hid)])],
        sems,
    )
    wait_all(copies[: 2 * blocks + 1])
    grad[...] = matmul(g_ref[...], down_ref[...], CONTRACT_LAST)
    wait_all(copies[2 * blocks + 1 :])
    pre[...] = matmul(x_ref[...], pair_ref[...])
    for at in range(0, hid, 128):
        cols = slice(at, at + 128)
        gate, up = pre[:, cols], pre[:, hid + at : hid + at + 128]
        hidden_grad = shift_tail(grad[:, cols], whole, -tail)
        first = first_rows(gate.shape, whole, tail)
        sig = 1.0 / (1.0 + jnp.exp(-gate))
        silu = gate * sig
        zero = jnp.zeros_like(gate)
        gate_grad = hidden_grad * up * sig * (1.0 + gate * (1.0 - sig))
        right_ref[:, at : at + 128] = jnp.where(first, gate_grad, zero).astype(jnp.bfloat16)
        right_ref[:, hid + at : hid + at + 128] = jnp.where(
            first, hidden_grad * silu, zero
        ).astype(jnp.bfloat16)
        hidden = shift_tail(jnp.where(first, silu * up, zero), whole, tail)
        hid_ref[:, cols] = hidden.astype(jnp.bfloat16)
    kept = pltpu.make_async_copy(right_ref, right_hbm, out_sems.at[3])
    kept.start()
    stores = []
    at, width = 0, out_ref.shape[0]
    while at < width:
        rows = min(1024 if at == 0 else 512, width - at)
        span = slice(at, at + rows)
        wide = matmul(x_ref[:, span], right_ref[...], CONTRACT_FIRST) * scale
        out_ref[span, : 2 * hid] = wide.astype(jnp.bfloat16)
        wide = matmul(g_ref[:, span], hid_ref[...], CONTRACT_FIRST) * scale
        out_ref[span, 2 * hid :] = wide.astype(jnp.bfloat16)
        part = pl.ds(at, rows)
        store = pltpu.make_async_copy(
            out_ref.at[part, :], partial_hbm.at[part, :], out_sems.at[len(stores)]
        )
        store.start()
        stores.append(store)
        at += rows
    wait_all(stores + [kept])


def expert_fwd(blocks, cap, recv_hbm, right_hbm, gate_hbm, up_hbm, down_hbm, out_hbm, rows_ref, right_ref, one_ref, two_ref, pair_ref, down_ref, low, high, hid_ref, sems, out_sems):
    hid = down_ref.shape[0]
    main, tail = split(cap)
    whole = blocks * main
    half = recv_hbm.shape[1]
    firsts, seconds, tails = sorted_rows(blocks, cap)
    low_cols, high_cols = pl.ds(0, half), pl.ds(half, half)
    copies = start_all(
        [(recv_hbm.at[source, :], rows_ref.at[target, low_cols]) for source, target in firsts + tails]
        + [(recv_hbm.at[source, :], rows_ref.at[target, high_cols]) for source, target in seconds + tails]
        + [(gate_hbm, pair_ref.at[:, pl.ds(0, hid)]), (up_hbm, pair_ref.at[:, pl.ds(hid, hid)])]
        + [(right_hbm, right_ref), (down_hbm, down_ref)],
        sems,
    )
    wait_all(copies[:-2])
    low[...] = matmul(rows_ref[:, :half], pair_ref[:half, :])
    high[...] = matmul(rows_ref[:, half:], pair_ref[half:, :])
    for at in range(0, hid, 128):
        cols = slice(at, at + 128)
        others = slice(hid + at, hid + at + 128)
        gate = low[:, cols] + shift_tail(high[:, cols], whole, -tail)
        up = low[:, others] + shift_tail(high[:, others], whole, -tail)
        hidden = gate / (1.0 + jnp.exp(-gate)) * up
        hidden = jnp.where(first_rows(gate.shape, whole, tail), hidden, jnp.zeros_like(hidden))
        hid_ref[:, cols] = shift_tail(hidden, whole, tail).astype(jnp.bfloat16)
    wait_all(copies[-2:])
    stores = []
    width = out_hbm.shape[1]
    span = width // 2
    for start in range(0, width, span):
        for at in range(start, start + span, CHUNK):
            cols = slice(at, at + CHUNK)
            one = matmul(right_ref[...], pair_ref[cols, :], CONTRACT_LAST)
            two = matmul(hid_ref[...], down_ref[:, cols])
            one_ref[:whole, cols] = one[:whole].astype(jnp.bfloat16)
            one_ref[whole:, cols] = (one[whole:] + two[whole:]).astype(jnp.bfloat16)
            two_ref[:, cols] = two[:whole].astype(jnp.bfloat16)
        part = pl.ds(start, span)
        for source, targets in ((one_ref, firsts), (two_ref, seconds), (one_ref, tails)):
            for target, rows in targets:
                copy = pltpu.make_async_copy(
                    source.at[rows, part], out_hbm.at[target, part], out_sems.at[len(stores)]
                )
                copy.start()
                stores.append(copy)
    wait_all(stores)


def widen(narrow_hbm, wide_hbm, narrow_ref, wide_ref, sems):
    parts = narrow_ref.shape[0] // 32
    spans = [pl.ds(i * 32, 32) for i in range(parts)]
    copies = start_all([(narrow_hbm.at[span, :], narrow_ref.at[span, :]) for span in spans], sems)
    stores = []
    for i, span in enumerate(spans):
        copies[i].wait()
        wide_ref[span, :] = narrow_ref[span, :].astype(jnp.float32)
        store = pltpu.make_async_copy(wide_ref.at[span, :], wide_hbm.at[span, :], sems.at[parts + i])
        store.start()
        stores.append(store)
    wait_all(stores)


def settle(one_hbm, two_hbm, one_out, two_out, one_ref, two_ref, sems):
    copies = start_all([(one_hbm, one_ref), (two_hbm, two_ref)], sems)
    stores = []
    for i, (held, target) in enumerate(((one_ref, one_out), (two_ref, two_out))):
        copies[i].wait()
        store = pltpu.make_async_copy(held, target, sems.at[2 + i])
        store.start()
        stores.append(store)
    wait_all(stores)


def as_column(row):
    count = row.shape[1]
    down = lax.broadcasted_iota(jnp.int32, (count, count), 0)
    across = lax.broadcasted_iota(jnp.int32, (count, count), 1)
    kept = jnp.where(down == across, jnp.broadcast_to(row, (count, count)), 0.0)
    return jnp.sum(kept, axis=1, keepdims=True)


def combine(experts, cap, back_hbm, fwd_ids_hbm, bwd_ids_hbm, gates_hbm, act_hbm, saved_hbm, grad_hbm, gain_hbm, act_out_hbm, grad_out_hbm, act_out_ref, grad_out_ref, back_ref, fwd_ids_ref, bwd_ids_ref, gates_ref, act_ref, saved_ref, grad_ref, gain_ref, wide, sems, out_sems):
    copies = start_all(
        [
            (fwd_ids_hbm, fwd_ids_ref),
            (bwd_ids_hbm, bwd_ids_ref),
            (gates_hbm, gates_ref),
            (back_hbm, back_ref),
            (saved_hbm, saved_ref),
            (gain_hbm, gain_ref),
            (act_hbm, act_ref),
            (grad_hbm, grad_ref),
        ],
        sems,
    )
    wait_all(copies[:3])
    tokens, width = act_ref.shape
    block = 2 * cap
    first, second = slots_of_rows(experts, cap, tokens)
    picks, _, before = slot_table(fwd_ids_ref[...], experts)
    chosen = [onehot(spread(jnp.where(pick, before, NOWHERE), block) == second) for pick in picks]
    gates = [as_column(gates_ref[k : k + 1, :]) for k in range(len(picks))]
    _, member, before = slot_table(bwd_ids_ref[...], experts)
    both = onehot(spread(jnp.where(member, before, NOWHERE), block) == first)
    wait_all(copies[3:])
    factor = row_factor(saved_ref)
    inner = jnp.zeros((tokens, 1), jnp.float32)
    for at in range(0, width, CHUNK):
        cols = slice(at, at + CHUNK)
        back = back_ref[:, cols]
        total = gates[0] * matmul(chosen[0], back, CONTRACT_FIRST)
        total = total + gates[1] * matmul(chosen[1], back, CONTRACT_FIRST)
        act_out_ref[:, cols] = (act_ref[:, cols].astype(jnp.float32) + total).astype(jnp.bfloat16)
        scaled = matmul(both, back, CONTRACT_FIRST) * gain_ref[:, cols]
        wide[:, cols] = scaled
        inner = inner + jnp.sum(
            saved_ref[:, cols].astype(jnp.float32) * scaled, axis=1, keepdims=True
        )
    stores = []
    store_columns(stores, act_out_ref, act_out_hbm, 0, width, out_sems)
    pull = inner / width * factor * factor * factor
    for at in range(0, width, CHUNK):
        cols = slice(at, at + CHUNK)
        value = grad_ref[:, cols].astype(jnp.float32) + (
            wide[:, cols] * factor - saved_ref[:, cols].astype(jnp.float32) * pull
        )
        grad_out_ref[:, cols] = value.astype(jnp.bfloat16)
        store_columns(stores, grad_out_ref, grad_out_hbm, at, CHUNK, out_sems)
    wait_all(stores)


PARAMS = pltpu.CompilerParams(vmem_limit_bytes=66_800_000)


def cost(flops, moved):
    return pl.CostEstimate(flops=flops, bytes_accessed=moved, transcendentals=0)


def exchange(rows, experts):
    blocks = rows.reshape(experts, -1, rows.shape[-1])
    moved = lax.all_to_all(blocks, "expert", split_axis=0, concat_axis=0, tiled=True)
    return moved.reshape(rows.shape)


def shards(
    act_in,
    saved_in,
    grad_in,
    fwd_ids,
    bwd_ids,
    fwd_gates,
    bwd_gates,
    norm_gain,
    w_gate,
    w_up,
    w_down,
):
    experts = lax.axis_size("expert")
    replicas = lax.axis_size("dp")
    sections = lax.axis_size("section")
    tokens, width = act_in.shape[1:]
    topk = fwd_ids.shape[2]
    cap = min(tokens, 5 * tokens * topk // (4 * experts))
    slots = 2 * cap * experts
    here, saved, upstream = act_in[0], saved_in[0], grad_in[0]
    weight_gate, weight_up, weight_down = w_gate[0, 0], w_up[0, 0], w_down[0, 0]
    hid = weight_gate.shape[1]
    ids_fwd, ids_bwd = fwd_ids[0].T, bwd_ids[0].T
    gates_fwd, gates_bwd = fwd_gates[0].T, bwd_gates[0].T
    small = tokens * width * 2
    big = slots * width * 2
    weight_bytes = 3 * width * hid * 2
    ids_buf = pltpu.VMEM((topk, tokens), jnp.int32)
    gates_buf = pltpu.VMEM((topk, tokens), jnp.float32)
    rows_buf = pltpu.VMEM((tokens, width), jnp.bfloat16)
    gain_buf = pltpu.VMEM((1, width), jnp.float32)
    slots_buf = pltpu.VMEM((slots, width), jnp.bfloat16)
    half_buf = pltpu.VMEM((slots, width // 2), jnp.bfloat16)
    main, tail = split(cap)
    rows = experts * (main + 2 * tail)
    sorted_buf = pltpu.VMEM((rows, width), jnp.bfloat16)
    right_buf = pltpu.VMEM((rows, 2 * hid), jnp.bfloat16)
    hid_buf = pltpu.VMEM((rows, hid), jnp.bfloat16)
    chunks = width // CHUNK
    dma = lambda count: pltpu.SemaphoreType.DMA((count,))
    weight_bufs = [
        pltpu.VMEM((width, 2 * hid), jnp.bfloat16),
        pltpu.VMEM((hid, width), jnp.bfloat16),
    ]

    send_bwd = pl.pallas_call(
        functools.partial(pack_bwd, experts, cap),
        out_shape=jax.ShapeDtypeStruct((slots, width), jnp.bfloat16),
        in_specs=[HBM] * 5,
        out_specs=HBM,
        scratch_shapes=[ids_buf, gates_buf, rows_buf, rows_buf, gain_buf, slots_buf, dma(5), dma(chunks)],
        compiler_params=PARAMS,
        cost_estimate=cost(4 * slots * tokens * width, 2 * small + big),
        name="pack_bwd",
    )(ids_bwd, gates_bwd, saved, upstream, norm_gain)
    recv_bwd = exchange(send_bwd, experts)
    send_fwd = pl.pallas_call(
        functools.partial(pack_fwd, experts, cap),
        out_shape=jax.ShapeDtypeStruct((slots, width // 2), jnp.bfloat16),
        in_specs=[HBM] * 3,
        out_specs=HBM,
        scratch_shapes=[ids_buf, rows_buf, gain_buf, half_buf, dma(3), dma(chunks)],
        compiler_params=PARAMS,
        cost_estimate=cost(2 * slots * tokens * width, small + big // 2),
        name="pack_fwd",
    )(ids_fwd, here, norm_gain)

    right, partial = pl.pallas_call(
        functools.partial(expert_bwd, experts, cap, 1.0 / replicas),
        out_shape=(
            jax.ShapeDtypeStruct((rows, 2 * hid), jnp.bfloat16),
            jax.ShapeDtypeStruct((width, 3 * hid), jnp.bfloat16),
        ),
        in_specs=[HBM] * 4,
        out_specs=(HBM, HBM),
        scratch_shapes=[sorted_buf, sorted_buf, right_buf, hid_buf]
        + weight_bufs
        + [pltpu.VMEM((rows, 2 * hid), jnp.float32), pltpu.VMEM((rows, hid), jnp.float32)]
        + [
            pltpu.VMEM((width, 3 * hid), jnp.bfloat16),
            dma(4 * experts + 3),
            dma(4),
        ],
        compiler_params=PARAMS,
        cost_estimate=cost(12 * slots * width * hid, big + 2 * weight_bytes),
        name="expert_bwd",
    )(recv_bwd, weight_gate, weight_up, weight_down)
    summed = lax.psum_scatter(partial, "dp", scatter_dimension=0, tiled=True)
    total = pl.pallas_call(
        widen,
        out_shape=jax.ShapeDtypeStruct(summed.shape, jnp.float32),
        in_specs=[HBM],
        out_specs=HBM,
        scratch_shapes=[
            pltpu.VMEM(summed.shape, jnp.bfloat16),
            pltpu.VMEM(summed.shape, jnp.float32),
            dma(2 * (summed.shape[0] // 32)),
        ],
        compiler_params=PARAMS,
        cost_estimate=cost(0, 6 * summed.size),
        name="widen",
    )(summed)

    send_fwd, right = lax.optimization_barrier((send_fwd, right))
    recv_fwd = exchange(send_fwd, experts)

    back = pl.pallas_call(
        functools.partial(expert_fwd, experts, cap),
        out_shape=jax.ShapeDtypeStruct((slots, width), jnp.bfloat16),
        in_specs=[HBM] * 5,
        out_specs=HBM,
        scratch_shapes=[sorted_buf, right_buf, sorted_buf, pltpu.VMEM((main * experts, width), jnp.bfloat16)]
        + weight_bufs
        + [pltpu.VMEM((rows, 2 * hid), jnp.float32)] * 2
        + [hid_buf, dma(4 * experts + 4), dma(6 * experts)],
        compiler_params=PARAMS,
        cost_estimate=cost(10 * slots * width * hid, 2 * big + weight_bytes),
        name="expert_fwd",
    )(recv_fwd, right, weight_gate, weight_up, weight_down)
    returned = exchange(back, experts)

    layer_out, input_grad = pl.pallas_call(
        functools.partial(combine, experts, cap),
        out_shape=(
            jax.ShapeDtypeStruct((tokens, width), jnp.bfloat16),
            jax.ShapeDtypeStruct((tokens, width), jnp.bfloat16),
        ),
        in_specs=[HBM] * 8,
        out_specs=(HBM, HBM),
        scratch_shapes=[rows_buf, rows_buf, slots_buf, ids_buf, ids_buf, gates_buf, rows_buf, rows_buf, rows_buf, gain_buf]
        + [pltpu.VMEM((tokens, width), jnp.float32), dma(8), dma(chunks + 1)],
        compiler_params=PARAMS,
        cost_estimate=cost(6 * slots * tokens * width, big + 5 * small),
        name="combine",
    )(returned, ids_fwd, ids_bwd, gates_fwd, here, saved, upstream, norm_gain)
    ring = [(i, (i + 1) % sections) for i in range(sections)]
    act_out = lax.ppermute(layer_out, "section", ring)
    grad_out = lax.ppermute(input_grad, "section", [(target, source) for source, target in ring])
    act_out, grad_out = pl.pallas_call(
        settle,
        out_shape=(
            jax.ShapeDtypeStruct(act_out.shape, act_out.dtype),
            jax.ShapeDtypeStruct(grad_out.shape, grad_out.dtype),
        ),
        in_specs=[HBM, HBM],
        out_specs=(HBM, HBM),
        scratch_shapes=[rows_buf, rows_buf, dma(4)],
        compiler_params=PARAMS,
        cost_estimate=cost(0, 4 * small),
        name="settle",
    )(act_out, grad_out)
    return (act_out[None], grad_out[None], total[None, None])


def solution(mesh):
    tokens = P("section", ("dp", "expert"), None)
    weights = P("section", "expert", None, None)
    in_specs = (tokens,) * 7 + (P("section", None),) + (weights,) * 3
    out_specs = (tokens, tokens, P("section", "expert", "dp", None))

    return jax.shard_map(shards, mesh=mesh, in_specs=in_specs, out_specs=out_specs, check_vma=False)
```
